32 devices in a mesh: space: 8 (over z, x), filt: 4 (over y, core).
Axes of the slice: x: 2, y: 2, z: 4, core: 2. Of those that a mesh axis runs over, the one named last changes fastest.
Arguments:
- inputs: bfloat16 [16, 4, 32, 512], P('space'), may hold values from -6 to 6
- pre_hidden: bfloat16 [16, 4, 32, 512], P('space'), may hold values from -6 to 6
- weight_one: bfloat16 [512, 3, 3, 3, 512], P(None, None, None, None, 'filt'), may hold values from -0.0546875 to 0.0546875
- weight_two: bfloat16 [512, 3, 3, 3, 512], P(None, None, None, None, 'filt'), may hold values from -0.0546875 to 0.0546875
- grad_out: bfloat16 [16, 4, 32, 512], P('space', None, None, 'filt'), may hold values from -6 to 6
Outputs:
- grad_inputs: bfloat16 [16, 4, 32, 512], P('space', 'filt')
- grad_one: float32 [512, 3, 3, 3, 512], P('space', None, None, None, 'filt')
- grad_two: float32 [512, 3, 3, 3, 512], P('space', None, None, None, 'filt')
The draws below stay inside these ranges and needn't reach their ends.
All inputs are finite; a program needn't handle non-finite values.
Results may differ from the reference program's by a relative error of at most 0.0049.
Values may be sent and summed in bfloat16 or wider, within the bound.
A program may use at most 128 MiB of HBM per device.

```python
import math
import jax
import jax.numpy as jnp
from jax import lax

CIN = 512
CMID = 512
COUT = 512
HEIGHT = 4
WIDTH = 32
DEPTH = 16


def with_spikes(drawn, stream_key, source, target, blocks, factor):
    def block_of(dim):
        return (jnp.arange(drawn.shape[dim]) // (drawn.shape[dim] // blocks)).reshape((-1,) + (1,) * (drawn.ndim - 1 - dim))

    near = jax.random.permutation(stream_key, blocks)[block_of(target)]
    other_side = (block_of(target) + blocks // 2) % blocks
    return jnp.where((block_of(source) == near) | (block_of(source) == other_side), factor * drawn, drawn)


def block_levels(rng, extent, cuts, smallest, largest):
    def one(position, shards_of):
        draws = jax.random.uniform(jax.random.fold_in(jax.random.fold_in(rng, 6), position), (shards_of,), jnp.float32, smallest / len(cuts), largest / len(cuts))
        return jnp.repeat(jnp.exp(draws), extent[position] // shards_of).reshape((-1,) + (1,) * (len(extent) - position - 1))

    gain = one(*cuts[0])
    for cut in cuts[1:]:
        gain = gain * one(*cut)
    return gain


def centred(stream_key, dims, scale, bound, shards=(), kind=jnp.bfloat16):
    values = jax.random.normal(stream_key, dims, jnp.float32) * scale
    if len(shards) > 0:
        values = block_levels(stream_key, dims, shards, -0.22, 0.18) * values
    return jnp.clip(values, min=-bound, max=bound).astype(kind)


def heavy_noise(own_key, shape, width, limit, shards, heavy, held_as=jnp.bfloat16):
    drawn = width * jax.random.normal(own_key, shape, jnp.float32)
    if shards:
        drawn = drawn * block_levels(own_key, shape, shards, -0.22, 0.18)
    return jnp.clip(with_spikes(drawn, jax.random.fold_in(own_key, 3), *heavy), -limit, limit).astype(held_as)


def setup_inputs(seed: int = 0) -> dict:
    keys = jax.random.split(jax.random.key(seed), 6)
    inputs = heavy_noise(keys[0], (DEPTH, HEIGHT, WIDTH, CIN), 1.0, 6.0, ((0, 8),), (0, 3, 8, 2.0))
    pre_hidden = heavy_noise(keys[1], (DEPTH, HEIGHT, WIDTH, CMID), 1.0, 6.0, ((0, 8),), (0, 3, 8, 2.0))
    weight_one = centred(keys[2], (CIN, 3, 3, 3, CMID), (27 * CIN) ** -0.5, 0.0546875, ((4, 4),))
    weight_two = centred(keys[3], (CMID, 3, 3, 3, COUT), (27 * CMID) ** -0.5, 0.0546875, ((4, 4),))
    grad_out = centred(keys[4], (DEPTH, HEIGHT, WIDTH, COUT), 1.0, 6.0, ((0, 8), (3, 4)))
    return dict(inputs=inputs, pre_hidden=pre_hidden, weight_one=weight_one, weight_two=weight_two, grad_out=grad_out)


TAP_LIST = [(tap_depth, tap_row, tap_col) for tap_depth in range(3) for tap_row in range(3) for tap_col in range(3)]

def window_at(padded, tap, planes, height, columns):
    return padded[2 - tap[0]:2 - tap[0] + planes, 2 - tap[1]:2 - tap[1] + height, 2 - tap[2]:2 - tap[2] + columns, :]

def carry_back(padded, weight, planes, height, columns):
    channels = weight.shape[4]
    summed = jnp.zeros((planes * height * columns, weight.shape[0]), jnp.float32)
    for tap in TAP_LIST:
        window = window_at(padded, tap, planes, height, columns).reshape(-1, channels)
        summed = summed + lax.dot_general(window, weight[:, tap[0], tap[1], tap[2], :], (((1,), (1,)), ((), ())), preferred_element_type=jnp.float32)
    return summed.reshape(planes, height, columns, weight.shape[0])

def weight_terms(source, padded, planes, height, columns):
    channels = padded.shape[3]
    pieces = []
    for tap in TAP_LIST:
        window = window_at(padded, tap, planes, height, columns).reshape(-1, channels)
        pieces.append(lax.dot_general(source, window, (((0,), (0,)), ((), ())), preferred_element_type=jnp.float32))
    return jnp.stack(pieces, axis=1).reshape(source.shape[1], 3, 3, 3, channels)

def reference(inputs, pre_hidden, weight_one, weight_two, grad_out):
    planes, height, columns, in_channels = inputs.shape
    voxel_count = planes * height * columns
    factor = 1.0 / math.sqrt(voxel_count)
    spread = ((1, 1), (1, 1), (1, 1), (0, 0))
    out_pad = jnp.pad(grad_out, spread)
    grad_hidden = carry_back(out_pad, weight_two, planes, height, columns)
    activity = jnp.maximum(pre_hidden, jnp.zeros_like(pre_hidden)).reshape(voxel_count, -1)
    grad_two = weight_terms(activity, out_pad, planes, height, columns) * factor
    grad_pre = jnp.where(pre_hidden > 0, grad_hidden, jnp.zeros_like(grad_hidden)).astype(jnp.bfloat16)
    pre_pad = jnp.pad(grad_pre, spread)
    grad_inputs = carry_back(pre_pad, weight_one, planes, height, columns).astype(jnp.bfloat16)
    grad_one = weight_terms(inputs.reshape(voxel_count, in_channels), pre_pad, planes, height, columns) * factor
    return (grad_inputs, grad_one, grad_two)
```

```python
import math

import jax
import jax.numpy as jnp
from jax import lax
from jax.sharding import PartitionSpec as P

TAP_LIST = [
    (tap_depth, tap_row, tap_col)
    for tap_depth in range(3)
    for tap_row in range(3)
    for tap_col in range(3)
]


def window_at(padded, tap, planes, height, columns):
    return padded[
        2 - tap[0] : 2 - tap[0] + planes,
        2 - tap[1] : 2 - tap[1] + height,
        2 - tap[2] : 2 - tap[2] + columns,
        :,
    ]


def carry_back(padded, weight, planes, height, columns):
    channels = weight.shape[4]
    summed = jnp.zeros((planes * height * columns, weight.shape[0]), jnp.float32)
    for tap in TAP_LIST:
        window = window_at(padded, tap, planes, height, columns).reshape(-1, channels)
        summed = summed + lax.dot_general(
            window,
            weight[:, tap[0], tap[1], tap[2], :],
            (((1,), (1,)), ((), ())),
            preferred_element_type=jnp.float32,
        )
    return summed.reshape(planes, height, columns, weight.shape[0])


def weight_terms(source, padded, planes, height, columns, factor):
    channels = padded.shape[3]
    pieces = []
    for tap in TAP_LIST:
        window = window_at(padded, tap, planes, height, columns).reshape(-1, channels)
        pieces.append(
            lax.dot_general(
                source, window, (((1,), (0,)), ((), ())), preferred_element_type=jnp.float32
            )
            * factor
        )
    return jnp.stack(pieces, axis=1).reshape(source.shape[0], 3, 3, 3, channels)


def pad_all(field):
    return jnp.pad(field, ((1, 1), (1, 1), (1, 1), (0, 0)))


def shards(inputs, pre_hidden, weight_one, weight_two, grad_out):
    planes, height, columns, in_channels = inputs.shape
    mid_channels = pre_hidden.shape[3]
    count = lax.axis_size("space")
    voxel_local = planes * height * columns
    factor = 1.0 / math.sqrt(voxel_local * count)
    start = lax.axis_index("space") * planes

    out_all = pad_all(lax.all_gather(grad_out, "space", axis=0, tiled=True))
    out_pad = lax.dynamic_slice_in_dim(out_all, start, planes + 2, 0)
    activity = jnp.maximum(pre_hidden, jnp.zeros_like(pre_hidden))
    both = jnp.stack([activity, inputs]).reshape(2, voxel_local, in_channels)
    both = jnp.swapaxes(both, 1, 2).reshape(2, count, in_channels // count, voxel_local)
    both = lax.all_to_all(both, "space", 1, 1)
    both = jnp.swapaxes(both, 1, 2).reshape(2, in_channels // count, count * voxel_local)

    hidden_partial = carry_back(out_pad, weight_two, planes, height, columns)
    grad_hidden = lax.psum_scatter(hidden_partial, "filt", scatter_dimension=3, tiled=True)
    group_width = grad_hidden.shape[3]
    own_pre = lax.dynamic_slice_in_dim(
        pre_hidden, lax.axis_index("filt") * group_width, group_width, 3
    )
    grad_pre = jnp.where(own_pre > 0, grad_hidden, jnp.zeros_like(grad_hidden)).astype(jnp.bfloat16)
    pre_all = pad_all(lax.all_gather(grad_pre, "space", axis=0, tiled=True))
    pre_pad = lax.dynamic_slice_in_dim(pre_all, start, planes + 2, 0)
    input_partial = carry_back(pre_pad, weight_one, planes, height, columns)
    grad_rows = lax.psum_scatter(input_partial, "filt", scatter_dimension=1, tiled=True)
    grad_inputs = grad_rows.astype(jnp.bfloat16)
    depth = planes * count
    grad_two = weight_terms(both[0], out_all, depth, height, columns, factor)
    grad_one = weight_terms(both[1], pre_all, depth, height, columns, factor)
    return (grad_inputs, grad_one, grad_two)


def solution(mesh):
    placed = (
        P("space", None, None, None),
        P("space", None, None, None),
        P(None, None, None, None, "filt"),
        P(None, None, None, None, "filt"),
        P("space", None, None, "filt"),
    )
    return jax.shard_map(
        shards,
        mesh=mesh,
        in_specs=placed,
        out_specs=(
            P("space", "filt", None, None),
            P("space", None, None, None, "filt"),
            P("space", None, None, None, "filt"),
        ),
        check_vma=False,
    )
```

```python
import functools
import math

import jax
import jax.numpy as jnp
from jax import lax
from jax.experimental import pallas as pl
from jax.experimental.pallas import tpu as pltpu
from jax.sharding import PartitionSpec as P

TAPS = 27
F32 = jnp.float32
BF16 = jnp.bfloat16
NT = (((1,), (1,)), ((), ()))


def kernel(
    cfg, act, grad, pre, w_one, w_two,
    gi, g_one, g_two,
    gall, pall, aall, slab, shifted, cols, wv_one, wv_two,
    send_one, recv_one, send_two, recv_two, part_two, lhs,
    w_sem, ag_s, ag_r, ap_s, ap_r, aa_s, aa_r, r1_s, r1_r, r2_s, r2_r,
):
    n, groups, planes, height, width, chan, factor = cfg
    area = height * width
    local = planes * area
    lanes = grad.shape[1]
    mid = w_two.shape[1]
    me = lax.axis_index("space")
    mine = lax.axis_index("filt")

    def w_copy(src, dst, t, s):
        return pltpu.make_async_copy(
            src.at[t], dst.at[:, pl.ds(t * lanes, lanes)], w_sem.at[s, t]
        )

    for t in range(TAPS):
        w_copy(w_two, wv_two, t, 1).start()

    barrier = pltpu.get_barrier_semaphore()

    def greet_space(k, c):
        pl.semaphore_signal(
            barrier, inc=1, device_id={"space": lax.rem(me + k, n)},
            device_id_type=pl.DeviceIdType.MESH,
        )
        return c

    lax.fori_loop(1, n, greet_space, 0)
    for k in range(1, groups):
        pl.semaphore_signal(
            barrier, inc=1, device_id={"filt": lax.rem(mine + k, groups)},
            device_id_type=pl.DeviceIdType.MESH,
        )
    pl.semaphore_wait(barrier, n + groups - 2)

    def over_space(src, dst, ss, rs, k):
        return pltpu.make_async_remote_copy(
            src_ref=src, dst_ref=dst, send_sem=ss, recv_sem=rs,
            device_id={"space": lax.rem(me + k, n)},
            device_id_type=pl.DeviceIdType.MESH,
        )

    def ag_out(k):
        return over_space(grad, gall.at[me], ag_s.at[k], ag_r.at[k], k)

    def ag_pre(k):
        return over_space(pall.at[me], pall.at[me], ap_s.at[k], ap_r.at[k], k)

    def ex_act(s, k):
        return over_space(
            act.at[s, lax.rem(me + k, n)], aall.at[s, me], aa_s.at[s, k], aa_r.at[s, k], k
        )

    def each(lo, hi, fn):
        def body(k, c):
            fn(k)
            return c

        lax.fori_loop(lo, hi, body, 0)

    ag_out(1).start()
    ag_out(n - 1).start()
    each(2, n - 1, lambda k: ag_out(k).start())
    each(1, n, lambda k: ex_act(0, k).start())
    for t in range(TAPS):
        w_copy(w_one, wv_one, t, 0).start()

    gall[me] = grad[...]
    aall[0, me] = act[0, me]
    aall[1, me] = act[1, me]
    shifted[...] = jnp.zeros_like(shifted)
    zero_plane = jnp.zeros((chan, area), BF16)
    for t in range(9):
        lhs[pl.ds(t * chan, chan), pl.ds(area, area)] = zero_plane
        lhs[pl.ds((18 + t) * chan, chan), pl.ds(n * planes * area, area)] = zero_plane

    def build_cols(field):
        below = field[lax.rem(me + n - 1, n), pl.ds(local - area, area), :]
        above = field[lax.rem(me + 1, n), pl.ds(0, area), :]
        slab[pl.ds(0, area), :] = jnp.where(me > 0, below.astype(F32), 0.0)
        slab[pl.ds(area, local), :] = field[me].astype(F32)
        slab[pl.ds(area + local, area), :] = jnp.where(me < n - 1, above.astype(F32), 0.0)
        whole = slab[...]
        rows = whole.shape[0]
        col = lax.rem(lax.broadcasted_iota(jnp.int32, whole.shape, 0), width)
        for c in range(3):
            moved = whole if c == 1 else pltpu.roll(whole, (c - 1) % rows, 0)
            if c == 0:
                moved = jnp.where(col < width - 1, moved, 0.0)
            if c == 2:
                moved = jnp.where(col > 0, moved, 0.0)
            shifted[c, :, pl.ds(1, height), :, :] = moved.astype(BF16).reshape(
                planes + 2, height, width, lanes
            )
        t = 0
        for a in range(3):
            for b in range(3):
                for c in range(3):
                    window = shifted[c, pl.ds(2 - a, planes), pl.ds(2 - b, height), :, :]
                    cols[:, pl.ds(t * lanes, lanes)] = window.reshape(local, lanes)
                    t += 1

    def build_lhs(s):
        lane = lax.broadcasted_iota(jnp.int32, (chan, local), 1)
        row = lax.rem(lane, area) // width
        col = lax.rem(lane, width)

        def body(j, carry):
            block = aall[s, j].astype(F32)
            for b in range(3):
                for c in range(3):
                    step = (b - 1) * width + (c - 1)
                    moved = block if step == 0 else pltpu.roll(block, (-step) % local, 1)
                    keep = None
                    if b != 1:
                        keep = (row > 0) if b == 0 else (row < height - 1)
                    if c != 1:
                        other = (col > 0) if c == 0 else (col < width - 1)
                        keep = other if keep is None else keep & other
                    if keep is not None:
                        moved = jnp.where(keep, moved, 0.0)
                    moved = moved.astype(BF16)
                    for a in range(3):
                        t = (a * 3 + b) * 3 + c
                        start = pl.multiple_of((j * planes + 2 - a) * area, area)
                        lhs[pl.ds(t * chan, chan), pl.ds(start, local)] = moved
            return carry

        lax.fori_loop(0, n, body, 0)

    def filter_grad(field, out):
        out[...] = jnp.zeros_like(out)

        def body(j, carry):
            start = pl.multiple_of((j * planes + 1) * area, area)
            out[...] += jnp.dot(
                lhs[:, pl.ds(start, local)], field[j], preferred_element_type=F32
            )
            return carry

        lax.fori_loop(0, n, body, 0)
        out[...] = out[...] * factor

    def over_filt(src, dst, ss, rs, k):
        return pltpu.make_async_remote_copy(
            src_ref=src, dst_ref=dst, send_sem=ss, recv_sem=rs,
            device_id={"filt": lax.rem(mine + k, groups)},
            device_id_type=pl.DeviceIdType.MESH,
        )

    def rs_one(k):
        return over_filt(
            send_one.at[k - 1], recv_one.at[k - 1], r1_s.at[k - 1], r1_r.at[k - 1], k
        )

    def rs_two(k):
        return over_filt(
            send_two.at[lax.rem(mine + k, groups)], recv_two.at[k - 1],
            r2_s.at[k - 1], r2_r.at[k - 1], k,
        )

    ag_out(1).wait_recv()
    ag_out(n - 1).wait_recv()
    build_cols(gall)
    for t in range(TAPS):
        w_copy(w_two, wv_two, t, 1).wait()
    share = mid // groups

    def hidden(group):
        start = pl.multiple_of(group * share, share)
        return lax.dot_general(
            cols[...], wv_two[pl.ds(start, share), :], NT, preferred_element_type=F32
        )

    for k in range(1, groups):
        send_one[k - 1] = hidden(lax.rem(mine + k, groups)).astype(BF16)
        rs_one(k).start()
    total = hidden(mine)
    for k in range(1, groups):
        rs_one(k).wait_recv()
        total = total + recv_one[k - 1].astype(F32)
    pall[me] = jnp.where(pre[...].astype(F32) > 0, total, 0.0).astype(BF16)
    ag_pre(1).start()
    ag_pre(n - 1).start()
    each(2, n - 1, lambda k: ag_pre(k).start())
    each(1, n, lambda k: ex_act(1, k).start())

    each(1, n, lambda k: ex_act(0, k).wait_recv())
    build_lhs(0)
    each(2, n - 1, lambda k: ag_out(k).wait_recv())
    filter_grad(gall, g_two)

    ag_pre(1).wait_recv()
    ag_pre(n - 1).wait_recv()
    build_cols(pall)
    for t in range(TAPS):
        w_copy(w_one, wv_one, t, 0).wait()
    rows = height // groups
    in_chan = w_one.shape[1]
    for q in range(in_chan // 128):
        piece = lax.dot_general(
            cols[...], wv_one[pl.ds(q * 128, 128), :], NT, preferred_element_type=F32
        ).reshape(planes, groups, rows * width, 128)
        for f in range(groups):
            for p in range(planes):
                part_two[f, pl.ds(p * rows * width, rows * width), pl.ds(q * 128, 128)] = piece[p, f]
    send_two[...] = part_two[...].astype(BF16)
    for k in range(1, groups):
        rs_two(k).start()

    each(1, n, lambda k: ex_act(1, k).wait_recv())
    build_lhs(1)
    each(2, n - 1, lambda k: ag_pre(k).wait_recv())
    filter_grad(pall, g_one)

    result = part_two[mine]
    for k in range(1, groups):
        rs_two(k).wait_recv()
        result = result + recv_two[k - 1].astype(F32)
    gi[...] = result.astype(BF16)

    for k in range(1, groups):
        rs_one(k).wait_send()
        rs_two(k).wait_send()

    def drain(k):
        ag_out(k).wait_send()
        ag_pre(k).wait_send()
        ex_act(0, k).wait_send()
        ex_act(1, k).wait_send()

    each(1, n, drain)


def shards(inputs, pre_hidden, weight_one, weight_two, grad_out):
    planes, height, width, in_chan = inputs.shape
    mid = pre_hidden.shape[3]
    lanes = grad_out.shape[3]
    n = lax.axis_size("space")
    groups = lax.axis_size("filt")
    area = height * width
    local = planes * area
    factor = 1.0 / math.sqrt(local * n)
    own = in_chan // n
    chan = max(own, 16)

    activity = jnp.maximum(pre_hidden, jnp.zeros_like(pre_hidden))
    act = jnp.stack([activity.reshape(local, mid), inputs.reshape(local, in_chan)])
    act = jnp.swapaxes(act, 1, 2).reshape(2, n, own, local)
    if chan != own:
        act = jnp.pad(act, ((0, 0), (0, 0), (0, chan - own), (0, 0)))
    share = mid // groups
    pre = lax.dynamic_slice_in_dim(
        pre_hidden.reshape(local, mid), lax.axis_index("filt") * share, share, 1
    )

    def tap_major(weight):
        return jnp.transpose(weight, (1, 2, 3, 0, 4)).reshape(TAPS, weight.shape[0], lanes)

    out_rows = planes * (height // groups) * width
    vmem = pl.BlockSpec(memory_space=pltpu.VMEM)
    hbm = pl.BlockSpec(memory_space=pl.ANY)
    dma = pltpu.SemaphoreType.DMA
    cfg = (n, groups, planes, height, width, chan, factor)
    gi, g_one, g_two = pl.pallas_call(
        functools.partial(kernel, cfg),
        out_shape=(
            jax.ShapeDtypeStruct((out_rows, in_chan), BF16),
            jax.ShapeDtypeStruct((TAPS * chan, lanes), F32),
            jax.ShapeDtypeStruct((TAPS * chan, lanes), F32),
        ),
        in_specs=[vmem, vmem, vmem, hbm, hbm],
        out_specs=(vmem, vmem, vmem),
        scratch_shapes=[
            pltpu.VMEM((n, local, lanes), BF16),
            pltpu.VMEM((n, local, lanes), BF16),
            pltpu.VMEM((2, n, chan, local), BF16),
            pltpu.VMEM((local + 2 * area, lanes), F32),
            pltpu.VMEM((3, planes + 2, height + 2, width, lanes), BF16),
            pltpu.VMEM((local, TAPS * lanes), BF16),
            pltpu.VMEM((in_chan, TAPS * lanes), BF16),
            pltpu.VMEM((mid, TAPS * lanes), BF16),
            pltpu.VMEM((groups - 1, local, share), BF16),
            pltpu.VMEM((groups - 1, local, share), BF16),
            pltpu.VMEM((groups, out_rows, in_chan), BF16),
            pltpu.VMEM((groups - 1, out_rows, in_chan), BF16),
            pltpu.VMEM((groups, out_rows, in_chan), F32),
            pltpu.VMEM((TAPS * chan, (n * planes + 2) * area), BF16),
            dma((2, TAPS)),
            dma((n,)), dma((n,)), dma((n,)), dma((n,)),
            dma((2, n)), dma((2, n)),
            dma((groups - 1,)), dma((groups - 1,)),
            dma((groups - 1,)), dma((groups - 1,)),
        ],
        compiler_params=pltpu.CompilerParams(
            collective_id=0, has_side_effects=True, vmem_limit_bytes=60 * 1024 * 1024
        ),
    )(act, grad_out.reshape(local, lanes), pre, tap_major(weight_one), tap_major(weight_two))

    def filters(g):
        g = g.reshape(3, 3, 3, chan, lanes)[:, :, :, :own, :]
        return jnp.transpose(g, (3, 0, 1, 2, 4))

    return gi.reshape(planes, height // groups, width, in_chan), filters(g_one), filters(g_two)


def solution(mesh):
    placed = (
        P("space", None, None, None),
        P("space", None, None, None),
        P(None, None, None, None, "filt"),
        P(None, None, None, None, "filt"),
        P("space", None, None, "filt"),
    )
    return jax.shard_map(
        shards,
        mesh=mesh,
        in_specs=placed,
        out_specs=(
            P("space", "filt", None, None),
            P("space", None, None, None, "filt"),
            P("space", None, None, None, "filt"),
        ),
        check_vma=False,
    )
```

```python
import functools
import math

import jax
import jax.numpy as jnp
from jax import lax
from jax.experimental import pallas as pl
from jax.experimental.pallas import tpu as pltpu
from jax.sharding import PartitionSpec as P

TAPS = 27
F32 = jnp.float32
BF16 = jnp.bfloat16
NT = (((1,), (1,)), ((), ()))


def kernel(
    cfg, source, hidden_in, grad, w_one, w_two,
    gi, g_one, g_two,
    act, gall, pall, aall, slab, shifted, cols, wv_one, wv_two,
    send_one, recv_one, send_two, recv_two, part_two, lhs,
    w_sem, ag_s, ag_r, ap_s, ap_r, aa_s, aa_r, r1_s, r1_r, r2_s, r2_r,
):
    n, groups, planes, height, width, chan, own = cfg
    area = height * width
    local = planes * area
    lanes = grad.shape[1]
    mid = w_two.shape[1]
    me = lax.axis_index("space")
    mine = lax.axis_index("filt")

    def w_copy(src, dst, t, s):
        return pltpu.make_async_copy(
            src.at[t], dst.at[:, pl.ds(t * lanes, lanes)], w_sem.at[s, t]
        )

    for t in range(TAPS):
        w_copy(w_two, wv_two, t, 1).start()

    barrier = pltpu.get_barrier_semaphore()

    def greet_space(k, c):
        pl.semaphore_signal(
            barrier, inc=1, device_id={"space": lax.rem(me + k, n)},
            device_id_type=pl.DeviceIdType.MESH,
        )
        return c

    lax.fori_loop(1, n, greet_space, 0)
    for k in range(1, groups):
        pl.semaphore_signal(
            barrier, inc=1, device_id={"filt": lax.rem(mine + k, groups)},
            device_id_type=pl.DeviceIdType.MESH,
        )
    pl.semaphore_wait(barrier, n + groups - 2)

    def over_space(src, dst, ss, rs, k):
        return pltpu.make_async_remote_copy(
            src_ref=src, dst_ref=dst, send_sem=ss, recv_sem=rs,
            device_id={"space": lax.rem(me + k, n)},
            device_id_type=pl.DeviceIdType.MESH,
        )

    partner = me + 1 - 2 * lax.rem(me, 2)
    evens = list(dict.fromkeys([2, n - 2] + list(range(4, n - 2, 2))))

    def origin(k):
        return lax.rem(me + n - k, n)

    def to_partner(src, dst, ss, rs):
        return pltpu.make_async_remote_copy(
            src_ref=src, dst_ref=dst, send_sem=ss, recv_sem=rs,
            device_id={"space": partner}, device_id_type=pl.DeviceIdType.MESH,
        )

    def gather(block, field, ss, rs):
        def direct(k):
            return over_space(block, field.at[me], ss.at[k], rs.at[me], k)

        def swap():
            return to_partner(block, field.at[me], ss.at[1], rs.at[me])

        def forward(k):
            j = origin(k)
            return to_partner(field.at[j], field.at[j], ss.at[k + 1], rs.at[j])

        def arrived(k):
            j = origin(k)
            to_partner(field.at[j], field.at[j], ss.at[0], rs.at[j]).wait_recv()

        def start():
            for k in evens[:2]:
                direct(k).start()
            swap().start()
            for k in evens[2:]:
                direct(k).start()

        def relay():
            for k in evens:
                arrived(k)
                forward(k).start()

        def finish():
            swap().wait_send()
            for k in evens:
                direct(k).wait_send()
                forward(k).wait_send()

        return start, relay, arrived, finish

    ag_start, ag_relay, ag_arrived, ag_finish = gather(grad, gall, ag_s, ag_r)
    ap_start, ap_relay, ap_arrived, ap_finish = gather(pall.at[me], pall, ap_s, ap_r)

    def ex_act(s, k):
        return over_space(
            act.at[s, lax.rem(me + k, n)], aall.at[s, me], aa_s.at[s, k], aa_r.at[s, k], k
        )

    def each(lo, hi, fn):
        def body(k, c):
            fn(k)
            return c

        lax.fori_loop(lo, hi, body, 0)

    ag_start()
    for t in range(TAPS):
        w_copy(w_one, wv_one, t, 0).start()

    gall[me] = grad[...]
    if chan != own:
        act[...] = jnp.zeros_like(act)
    for s, ref in enumerate((hidden_in, source)):
        wide = ref[...].astype(F32)
        if s == 0:
            wide = jnp.maximum(wide, 0.0)
        wide = wide.T
        for j in range(n):
            act[s, j, pl.ds(0, own), :] = wide[j * own : (j + 1) * own].astype(BF16)
    ag_relay()
    each(1, n, lambda k: ex_act(0, k).start())
    aall[0, me] = act[0, me]
    aall[1, me] = act[1, me]
    shifted[...] = jnp.zeros_like(shifted)
    zero_plane = jnp.zeros((chan, area), BF16)
    for t in range(9):
        lhs[pl.ds(t * chan, chan), pl.ds(area, area)] = zero_plane
        lhs[pl.ds((18 + t) * chan, chan), pl.ds(n * planes * area, area)] = zero_plane

    def build_cols(field):
        below = field[lax.rem(me + n - 1, n), pl.ds(local - area, area), :]
        above = field[lax.rem(me + 1, n), pl.ds(0, area), :]
        slab[pl.ds(0, area), :] = jnp.where(me > 0, below.astype(F32), 0.0)
        slab[pl.ds(area, local), :] = field[me].astype(F32)
        slab[pl.ds(area + local, area), :] = jnp.where(me < n - 1, above.astype(F32), 0.0)
        whole = slab[...]
        rows = whole.shape[0]
        col = lax.rem(lax.broadcasted_iota(jnp.int32, whole.shape, 0), width)
        for c in range(3):
            moved = whole if c == 1 else pltpu.roll(whole, (c - 1) % rows, 0)
            if c == 0:
                moved = jnp.where(col < width - 1, moved, 0.0)
            if c == 2:
                moved = jnp.where(col > 0, moved, 0.0)
            shifted[c, :, pl.ds(1, height), :, :] = moved.astype(BF16).reshape(
                planes + 2, height, width, lanes
            )
        t = 0
        for a in range(3):
            for b in range(3):
                for c in range(3):
                    window = shifted[c, pl.ds(2 - a, planes), pl.ds(2 - b, height), :, :]
                    cols[:, pl.ds(t * lanes, lanes)] = window.reshape(local, lanes)
                    t += 1

    def build_lhs(s):
        lane = lax.broadcasted_iota(jnp.int32, (chan, local), 1)
        row = lax.rem(lane, area) // width
        col = lax.rem(lane, width)

        def body(j, carry):
            block = aall[s, j].astype(F32)
            for b in range(3):
                for c in range(3):
                    step = (b - 1) * width + (c - 1)
                    moved = block if step == 0 else pltpu.roll(block, (-step) % local, 1)
                    keep = None
                    if b != 1:
                        keep = (row > 0) if b == 0 else (row < height - 1)
                    if c != 1:
                        other = (col > 0) if c == 0 else (col < width - 1)
                        keep = other if keep is None else keep & other
                    if keep is not None:
                        moved = jnp.where(keep, moved, 0.0)
                    moved = moved.astype(BF16)
                    for a in range(3):
                        t = (a * 3 + b) * 3 + c
                        start = pl.multiple_of((j * planes + 2 - a) * area, area)
                        lhs[pl.ds(t * chan, chan), pl.ds(start, local)] = moved
            return carry

        lax.fori_loop(0, n, body, 0)

    def filter_grad(field, out):
        out[...] = jnp.zeros_like(out)

        def body(j, carry):
            start = pl.multiple_of((j * planes + 1) * area, area)
            out[...] += jnp.dot(
                lhs[:, pl.ds(start, local)], field[j], preferred_element_type=F32
            )
            return carry

        lax.fori_loop(0, n, body, 0)

    def over_filt(src, dst, ss, rs, k):
        return pltpu.make_async_remote_copy(
            src_ref=src, dst_ref=dst, send_sem=ss, recv_sem=rs,
            device_id={"filt": lax.rem(mine + k, groups)},
            device_id_type=pl.DeviceIdType.MESH,
        )

    def rs_one(k):
        return over_filt(
            send_one.at[k - 1], recv_one.at[k - 1], r1_s.at[k - 1], r1_r.at[k - 1], k
        )

    def rs_two(k):
        return over_filt(
            send_two.at[lax.rem(mine + k, groups)], recv_two.at[k - 1],
            r2_s.at[k - 1], r2_r.at[k - 1], k,
        )

    ag_arrived(1)
    ag_arrived(n - 1)
    build_cols(gall)
    for t in range(TAPS):
        w_copy(w_two, wv_two, t, 1).wait()
    share = mid // groups

    def hidden(group):
        start = pl.multiple_of(group * share, share)
        return lax.dot_general(
            cols[...], wv_two[pl.ds(start, share), :], NT, preferred_element_type=F32
        )

    for k in range(1, groups):
        send_one[k - 1] = hidden(lax.rem(mine + k, groups)).astype(BF16)
        rs_one(k).start()
    total = hidden(mine)
    for k in range(1, groups):
        rs_one(k).wait_recv()
        total = total + recv_one[k - 1].astype(F32)
    own_pre = hidden_in[:, pl.ds(pl.multiple_of(mine * share, share), share)]
    pall[me] = jnp.where(own_pre.astype(F32) > 0, total, 0.0).astype(BF16)
    ap_start()

    each(1, n, lambda k: ex_act(0, k).wait_recv())
    build_lhs(0)
    ap_relay()
    each(1, n, lambda k: ex_act(1, k).start())
    for k in range(3, n - 2, 2):
        ag_arrived(k)
    filter_grad(gall, g_two)

    ap_arrived(1)
    ap_arrived(n - 1)
    build_cols(pall)
    for t in range(TAPS):
        w_copy(w_one, wv_one, t, 0).wait()
    rows = height // groups
    in_chan = w_one.shape[1]
    for q in range(in_chan // 128):
        piece = lax.dot_general(
            cols[...], wv_one[pl.ds(q * 128, 128), :], NT, preferred_element_type=F32
        ).reshape(planes, groups, rows * width, 128)
        for f in range(groups):
            for p in range(planes):
                part_two[f, pl.ds(p * rows * width, rows * width), pl.ds(q * 128, 128)] = piece[p, f]
    send_two[...] = part_two[...].astype(BF16)
    for k in range(1, groups):
        rs_two(k).start()

    each(1, n, lambda k: ex_act(1, k).wait_recv())
    build_lhs(1)
    for k in range(3, n - 2, 2):
        ap_arrived(k)
    filter_grad(pall, g_one)

    result = part_two[mine]
    for k in range(1, groups):
        rs_two(k).wait_recv()
        result = result + recv_two[k - 1].astype(F32)
    gi[...] = result.astype(BF16)

    for k in range(1, groups):
        rs_one(k).wait_send()
        rs_two(k).wait_send()

    def drain(k):
        ex_act(0, k).wait_send()
        ex_act(1, k).wait_send()

    each(1, n, drain)
    ag_finish()
    ap_finish()


def shards(inputs, pre_hidden, weight_one, weight_two, grad_out):
    planes, height, width, in_chan = inputs.shape
    mid = pre_hidden.shape[3]
    lanes = grad_out.shape[3]
    n = lax.axis_size("space")
    groups = lax.axis_size("filt")
    area = height * width
    local = planes * area
    factor = 1.0 / math.sqrt(local * n)
    own = in_chan // n
    chan = max(own, 16)

    share = mid // groups

    def tap_major(weight):
        return jnp.transpose(weight, (1, 2, 3, 0, 4)).reshape(TAPS, weight.shape[0], lanes)

    out_rows = planes * (height // groups) * width
    vmem = pl.BlockSpec(memory_space=pltpu.VMEM)
    hbm = pl.BlockSpec(memory_space=pl.ANY)
    dma = pltpu.SemaphoreType.DMA
    cfg = (n, groups, planes, height, width, chan, own)
    gi, g_one, g_two = pl.pallas_call(
        functools.partial(kernel, cfg),
        out_shape=(
            jax.ShapeDtypeStruct((out_rows, in_chan), BF16),
            jax.ShapeDtypeStruct((TAPS * chan, lanes), F32),
            jax.ShapeDtypeStruct((TAPS * chan, lanes), F32),
        ),
        in_specs=[vmem, vmem, vmem, hbm, hbm],
        out_specs=(vmem, vmem, vmem),
        scratch_shapes=[
            pltpu.VMEM((2, n, chan, local), BF16),
            pltpu.VMEM((n, local, lanes), BF16),
            pltpu.VMEM((n, local, lanes), BF16),
            pltpu.VMEM((2, n, chan, local), BF16),
            pltpu.VMEM((local + 2 * area, lanes), F32),
            pltpu.VMEM((3, planes + 2, height + 2, width, lanes), BF16),
            pltpu.VMEM((local, TAPS * lanes), BF16),
            pltpu.VMEM((in_chan, TAPS * lanes), BF16),
            pltpu.VMEM((mid, TAPS * lanes), BF16),
            pltpu.VMEM((groups - 1, local, share), BF16),
            pltpu.VMEM((groups - 1, local, share), BF16),
            pltpu.VMEM((groups, out_rows, in_chan), BF16),
            pltpu.VMEM((groups - 1, out_rows, in_chan), BF16),
            pltpu.VMEM((groups, out_rows, in_chan), F32),
            pltpu.VMEM((TAPS * chan, (n * planes + 2) * area), BF16),
            dma((2, TAPS)),
            dma((n,)), dma((n,)), dma((n,)), dma((n,)),
            dma((2, n)), dma((2, n)),
            dma((groups - 1,)), dma((groups - 1,)),
            dma((groups - 1,)), dma((groups - 1,)),
        ],
        compiler_params=pltpu.CompilerParams(
            collective_id=0, has_side_effects=True, vmem_limit_bytes=60 * 1024 * 1024
        ),
    )(
        inputs.reshape(local, in_chan), pre_hidden.reshape(local, mid),
        grad_out.reshape(local, lanes), tap_major(weight_one), tap_major(weight_two),
    )

    def filters(g):
        g = (g * factor).reshape(3, 3, 3, chan, lanes)[:, :, :, :own, :]
        return jnp.transpose(g, (3, 0, 1, 2, 4))

    return gi.reshape(planes, height // groups, width, in_chan), filters(g_one), filters(g_two)


def solution(mesh):
    placed = (
        P("space", None, None, None),
        P("space", None, None, None),
        P(None, None, None, None, "filt"),
        P(None, None, None, None, "filt"),
        P("space", None, None, "filt"),
    )
    return jax.shard_map(
        shards,
        mesh=mesh,
        in_specs=placed,
        out_specs=(
            P("space", "filt", None, None),
            P("space", None, None, None, "filt"),
            P("space", None, None, None, "filt"),
        ),
        check_vma=False,
    )
```

```python
import functools
import math

import jax
import jax.numpy as jnp
from jax import lax
from jax.experimental import pallas as pl
from jax.experimental.pallas import tpu as pltpu
from jax.sharding import PartitionSpec as P

TAPS = 27
F32 = jnp.float32
BF16 = jnp.bfloat16
NT = (((1,), (1,)), ((), ()))


def kernel(
    cfg, source, hidden_in, grad, w_one, w_two,
    gi, g_one, g_two,
    act, gall, pall, aall, slab, shifted, cols, wv_one, wv_two,
    send_one, recv_one, send_two, recv_two, part_two, lhs,
    w_sem, ag_s, ag_r, ap_s, ap_r, aa_s, aa_r, r1_s, r1_r, r2_s, r2_r,
):
    n, groups, planes, height, width, chan, own = cfg
    area = height * width
    local = planes * area
    lanes = grad.shape[1]
    mid = w_two.shape[1]
    me = lax.axis_index("space")
    mine = lax.axis_index("filt")

    def w_copy(src, dst, t, s):
        return pltpu.make_async_copy(
            src.at[t], dst.at[:, pl.ds(t * lanes, lanes)], w_sem.at[s, t]
        )

    for t in range(TAPS):
        w_copy(w_two, wv_two, t, 1).start()

    barrier = pltpu.get_barrier_semaphore()

    def greet_space(k, c):
        pl.semaphore_signal(
            barrier, inc=1, device_id={"space": lax.rem(me + k, n)},
            device_id_type=pl.DeviceIdType.MESH,
        )
        return c

    lax.fori_loop(1, n, greet_space, 0)
    for k in range(1, groups):
        pl.semaphore_signal(
            barrier, inc=1, device_id={"filt": lax.rem(mine + k, groups)},
            device_id_type=pl.DeviceIdType.MESH,
        )
    pl.semaphore_wait(barrier, n + groups - 2)

    def over_space(src, dst, ss, rs, k):
        return pltpu.make_async_remote_copy(
            src_ref=src, dst_ref=dst, send_sem=ss, recv_sem=rs,
            device_id={"space": lax.rem(me + k, n)},
            device_id_type=pl.DeviceIdType.MESH,
        )

    partner = me + 1 - 2 * lax.rem(me, 2)
    evens = list(dict.fromkeys([2, n - 2] + list(range(4, n - 2, 2))))

    def origin(k):
        return lax.rem(me + n - k, n)

    def to_partner(src, dst, ss, rs):
        return pltpu.make_async_remote_copy(
            src_ref=src, dst_ref=dst, send_sem=ss, recv_sem=rs,
            device_id={"space": partner}, device_id_type=pl.DeviceIdType.MESH,
        )

    def gather(block, field, ss, rs):
        def direct(k):
            return over_space(block, field.at[me], ss.at[k], rs.at[me], k)

        def swap():
            return to_partner(block, field.at[me], ss.at[1], rs.at[me])

        def forward(k):
            j = origin(k)
            return to_partner(field.at[j], field.at[j], ss.at[k + 1], rs.at[j])

        def arrived(k):
            j = origin(k)
            to_partner(field.at[j], field.at[j], ss.at[0], rs.at[j]).wait_recv()

        def start():
            for k in evens[:2]:
                direct(k).start()
            swap().start()
            for k in evens[2:]:
                direct(k).start()

        def relay():
            for k in evens:
                arrived(k)
                forward(k).start()

        def finish():
            swap().wait_send()
            for k in evens:
                direct(k).wait_send()
                forward(k).wait_send()

        return start, relay, arrived, finish

    ag_start, ag_relay, ag_arrived, ag_finish = gather(grad, gall, ag_s, ag_r)
    ap_start, ap_relay, ap_arrived, ap_finish = gather(pall.at[me], pall, ap_s, ap_r)

    def ex_act(s, k):
        return over_space(
            act.at[s, lax.rem(me + k, n)], aall.at[s, me], aa_s.at[s, k], aa_r.at[s, k], k
        )

    def each(lo, hi, fn):
        def body(k, c):
            fn(k)
            return c

        lax.fori_loop(lo, hi, body, 0)

    ag_start()
    for t in range(TAPS):
        w_copy(w_one, wv_one, t, 0).start()

    gall[me] = grad[...]
    if chan != own:
        act[...] = jnp.zeros_like(act)
    for s, ref in enumerate((hidden_in, source)):
        wide = ref[...].astype(F32)
        if s == 0:
            wide = jnp.maximum(wide, 0.0)
        wide = wide.T
        for j in range(n):
            act[s, j, pl.ds(0, own), :] = wide[j * own : (j + 1) * own].astype(BF16)
    ag_relay()
    each(1, n, lambda k: ex_act(0, k).start())
    aall[0, me] = act[0, me]
    aall[1, me] = act[1, me]
    shifted[...] = jnp.zeros_like(shifted)
    zero_plane = jnp.zeros((chan, area), BF16)
    for t in range(9):
        lhs[pl.ds(t * chan, chan), pl.ds(area, area)] = zero_plane
        lhs[pl.ds((18 + t) * chan, chan), pl.ds(n * planes * area, area)] = zero_plane

    def build_cols(field):
        below = field[lax.rem(me + n - 1, n), pl.ds(local - area, area), :]
        above = field[lax.rem(me + 1, n), pl.ds(0, area), :]
        slab[pl.ds(0, area), :] = jnp.where(me > 0, below.astype(F32), 0.0)
        slab[pl.ds(area, local), :] = field[me].astype(F32)
        slab[pl.ds(area + local, area), :] = jnp.where(me < n - 1, above.astype(F32), 0.0)
        whole = slab[...]
        rows = whole.shape[0]
        col = lax.rem(lax.broadcasted_iota(jnp.int32, whole.shape, 0), width)
        for c in range(3):
            moved = whole if c == 1 else pltpu.roll(whole, (c - 1) % rows, 0)
            if c == 0:
                moved = jnp.where(col < width - 1, moved, 0.0)
            if c == 2:
                moved = jnp.where(col > 0, moved, 0.0)
            shifted[c, :, pl.ds(1, height), :, :] = moved.astype(BF16).reshape(
                planes + 2, height, width, lanes
            )
        t = 0
        for a in range(3):
            for b in range(3):
                for c in range(3):
                    window = shifted[c, pl.ds(2 - a, planes), pl.ds(2 - b, height), :, :]
                    cols[:, pl.ds(t * lanes, lanes)] = window.reshape(local, lanes)
                    t += 1

    def build_lhs(s):
        lane = lax.broadcasted_iota(jnp.int32, (chan, local), 1)
        row = lax.rem(lane, area) // width
        col = lax.rem(lane, width)

        def body(j, carry):
            block = aall[s, j].astype(F32)
            for b in range(3):
                for c in range(3):
                    step = (b - 1) * width + (c - 1)
                    moved = block if step == 0 else pltpu.roll(block, (-step) % local, 1)
                    keep = None
                    if b != 1:
                        keep = (row > 0) if b == 0 else (row < height - 1)
                    if c != 1:
                        other = (col > 0) if c == 0 else (col < width - 1)
                        keep = other if keep is None else keep & other
                    if keep is not None:
                        moved = jnp.where(keep, moved, 0.0)
                    moved = moved.astype(BF16)
                    for a in range(3):
                        t = (a * 3 + b) * 3 + c
                        start = pl.multiple_of((j * planes + 2 - a) * area, area)
                        lhs[pl.ds(t * chan, chan), pl.ds(start, local)] = moved
            return carry

        lax.fori_loop(0, n, body, 0)

    def filter_grad(field, out):
        out[...] = jnp.zeros_like(out)

        def body(j, carry):
            start = pl.multiple_of((j * planes + 1) * area, area)
            out[...] += jnp.dot(
                lhs[:, pl.ds(start, local)], field[j], preferred_element_type=F32
            )
            return carry

        lax.fori_loop(0, n, body, 0)

    def over_filt(src, dst, ss, rs, k):
        return pltpu.make_async_remote_copy(
            src_ref=src, dst_ref=dst, send_sem=ss, recv_sem=rs,
            device_id={"filt": lax.rem(mine + k, groups)},
            device_id_type=pl.DeviceIdType.MESH,
        )

    def rs_one(k):
        return over_filt(
            send_one.at[k - 1], recv_one.at[k - 1], r1_s.at[k - 1], r1_r.at[k - 1], k
        )

    def rs_two(k):
        return over_filt(
            send_two.at[lax.rem(mine + k, groups)], recv_two.at[k - 1],
            r2_s.at[k - 1], r2_r.at[k - 1], k,
        )

    ag_arrived(1)
    ag_arrived(n - 1)
    build_cols(gall)
    for t in range(TAPS):
        w_copy(w_two, wv_two, t, 1).wait()
    share = mid // groups

    def hidden(group):
        start = pl.multiple_of(group * share, share)
        return lax.dot_general(
            cols[...], wv_two[pl.ds(start, share), :], NT, preferred_element_type=F32
        )

    for k in range(1, groups):
        send_one[k - 1] = hidden(lax.rem(mine + k, groups)).astype(BF16)
        rs_one(k).start()
    total = hidden(mine)
    each(1, n, lambda k: ex_act(0, k).wait_recv())
    build_lhs(0)
    for k in range(1, groups):
        rs_one(k).wait_recv()
        total = total + recv_one[k - 1].astype(F32)
    own_pre = hidden_in[:, pl.ds(pl.multiple_of(mine * share, share), share)]
    pall[me] = jnp.where(own_pre.astype(F32) > 0, total, 0.0).astype(BF16)
    ap_start()

    for k in range(3, n - 2, 2):
        ag_arrived(k)
    filter_grad(gall, g_two)
    ap_relay()
    each(1, n, lambda k: ex_act(1, k).start())

    ap_arrived(1)
    ap_arrived(n - 1)
    build_cols(pall)
    for t in range(TAPS):
        w_copy(w_one, wv_one, t, 0).wait()
    rows = height // groups
    in_chan = w_one.shape[1]
    for q in range(in_chan // 128):
        piece = lax.dot_general(
            cols[...], wv_one[pl.ds(q * 128, 128), :], NT, preferred_element_type=F32
        ).reshape(planes, groups, rows * width, 128)
        for f in range(groups):
            for p in range(planes):
                part_two[f, pl.ds(p * rows * width, rows * width), pl.ds(q * 128, 128)] = piece[p, f]
    send_two[...] = part_two[...].astype(BF16)
    for k in range(1, groups):
        rs_two(k).start()

    each(1, n, lambda k: ex_act(1, k).wait_recv())
    build_lhs(1)
    for k in range(3, n - 2, 2):
        ap_arrived(k)
    filter_grad(pall, g_one)

    result = part_two[mine]
    for k in range(1, groups):
        rs_two(k).wait_recv()
        result = result + recv_two[k - 1].astype(F32)
    gi[...] = result.astype(BF16)

    for k in range(1, groups):
        rs_one(k).wait_send()
        rs_two(k).wait_send()

    def drain(k):
        ex_act(0, k).wait_send()
        ex_act(1, k).wait_send()

    each(1, n, drain)
    ag_finish()
    ap_finish()


def shards(inputs, pre_hidden, weight_one, weight_two, grad_out):
    planes, height, width, in_chan = inputs.shape
    mid = pre_hidden.shape[3]
    lanes = grad_out.shape[3]
    n = lax.axis_size("space")
    groups = lax.axis_size("filt")
    area = height * width
    local = planes * area
    factor = 1.0 / math.sqrt(local * n)
    own = in_chan // n
    chan = max(own, 16)

    share = mid // groups

    def tap_major(weight):
        return jnp.transpose(weight, (1, 2, 3, 0, 4)).reshape(TAPS, weight.shape[0], lanes)

    out_rows = planes * (height // groups) * width
    vmem = pl.BlockSpec(memory_space=pltpu.VMEM)
    hbm = pl.BlockSpec(memory_space=pl.ANY)
    dma = pltpu.SemaphoreType.DMA
    cfg = (n, groups, planes, height, width, chan, own)
    gi, g_one, g_two = pl.pallas_call(
        functools.partial(kernel, cfg),
        out_shape=(
            jax.ShapeDtypeStruct((out_rows, in_chan), BF16),
            jax.ShapeDtypeStruct((TAPS * chan, lanes), F32),
            jax.ShapeDtypeStruct((TAPS * chan, lanes), F32),
        ),
        in_specs=[vmem, vmem, vmem, hbm, hbm],
        out_specs=(vmem, vmem, vmem),
        scratch_shapes=[
            pltpu.VMEM((2, n, chan, local), BF16),
            pltpu.VMEM((n, local, lanes), BF16),
            pltpu.VMEM((n, local, lanes), BF16),
            pltpu.VMEM((2, n, chan, local), BF16),
            pltpu.VMEM((local + 2 * area, lanes), F32),
            pltpu.VMEM((3, planes + 2, height + 2, width, lanes), BF16),
            pltpu.VMEM((local, TAPS * lanes), BF16),
            pltpu.VMEM((in_chan, TAPS * lanes), BF16),
            pltpu.VMEM((mid, TAPS * lanes), BF16),
            pltpu.VMEM((groups - 1, local, share), BF16),
            pltpu.VMEM((groups - 1, local, share), BF16),
            pltpu.VMEM((groups, out_rows, in_chan), BF16),
            pltpu.VMEM((groups - 1, out_rows, in_chan), BF16),
            pltpu.VMEM((groups, out_rows, in_chan), F32),
            pltpu.VMEM((TAPS * chan, (n * planes + 2) * area), BF16),
            dma((2, TAPS)),
            dma((n,)), dma((n,)), dma((n,)), dma((n,)),
            dma((2, n)), dma((2, n)),
            dma((groups - 1,)), dma((groups - 1,)),
            dma((groups - 1,)), dma((groups - 1,)),
        ],
        compiler_params=pltpu.CompilerParams(
            collective_id=0, has_side_effects=True, vmem_limit_bytes=60 * 1024 * 1024
        ),
    )(
        inputs.reshape(local, in_chan), pre_hidden.reshape(local, mid),
        grad_out.reshape(local, lanes), tap_major(weight_one), tap_major(weight_two),
    )

    def filters(g):
        g = (g * factor).reshape(3, 3, 3, chan, lanes)[:, :, :, :own, :]
        return jnp.transpose(g, (3, 0, 1, 2, 4))

    return gi.reshape(planes, height // groups, width, in_chan), filters(g_one), filters(g_two)


def solution(mesh):
    placed = (
        P("space", None, None, None),
        P("space", None, None, None),
        P(None, None, None, None, "filt"),
        P(None, None, None, None, "filt"),
        P("space", None, None, "filt"),
    )
    return jax.shard_map(
        shards,
        mesh=mesh,
        in_specs=placed,
        out_specs=(
            P("space", "filt", None, None),
            P("space", None, None, None, "filt"),
            P("space", None, None, None, "filt"),
        ),
        check_vma=False,
    )
```
